128 devices in a mesh: shard: 16 (over y, z), tensor: 4 (over x), section: 2 (over core).
Axes of the slice: x: 4, y: 4, z: 4, core: 2. Of those that a mesh axis runs over, the one named last changes fastest.
Arguments:
- attention_grads: float32 [16, 4, 768, 768], P('shard', 'section', 'tensor'), may hold values from -48 to 48
- feedforward_grads: float32 [16, 2, 3072, 768], P('shard', 'section', 'tensor'), may hold values from -48 to 48
- attention_errors: float32 [16, 4, 768, 768], P('shard', 'section', 'tensor'), may hold values from -3 to 3
- feedforward_errors: float32 [16, 2, 3072, 768], P('shard', 'section', 'tensor'), may hold values from -3 to 3
- attention_factor: float32 [4, 768, 32], P('section'), may hold values from -0.21875 to 0.21875
- feedforward_factor: float32 [2, 768, 32], P('section'), may hold values from -0.21875 to 0.21875
- attention_momentum: float32 [4, 768, 768], P('section', 'tensor', 'shard'), may hold values from -3 to 3
- feedforward_momentum: float32 [2, 3072, 768], P('section', 'tensor', 'shard'), may hold values from -3 to 3
- attention_master: float32 [4, 768, 768], P('section', 'tensor', 'shard'), may hold values from -3 to 3
- feedforward_master: float32 [2, 3072, 768], P('section', 'tensor', 'shard'), may hold values from -3 to 3
- gain_grads: float32 [16, 2, 768], P('shard', 'section', 'tensor'), may hold values from -6 to 6
- bias_grads: float32 [16, 12, 32], P('shard', 'tensor'), may hold values from -6 to 6
- gain_momentum: float32 [2, 768], P('section', 'tensor'), may hold values from -3 to 3
- gain_weight: float32 [2, 768], P('section', 'tensor'), may hold values from 0.5 to 1.5
- bias_momentum: float32 [12, 32], P('tensor'), may hold values from -3 to 3
- bias_weight: float32 [12, 32], P('tensor'), may hold values from -4 to 4
Outputs:
- attention_errors_new: float32 [16, 4, 768, 768], P('shard', 'section', 'tensor')
- feedforward_errors_new: float32 [16, 2, 3072, 768], P('shard', 'section', 'tensor')
- attention_factor_new: float32 [4, 768, 32], P('section')
- feedforward_factor_new: float32 [2, 768, 32], P('section')
- attention_momentum_new: float32 [4, 768, 768], P('section', 'tensor', 'shard')
- feedforward_momentum_new: float32 [2, 3072, 768], P('section', 'tensor', 'shard')
- attention_master_new: float32 [4, 768, 768], P('section', 'tensor', 'shard')
- feedforward_master_new: float32 [2, 3072, 768], P('section', 'tensor', 'shard')
- attention_fresh: bfloat16 [4, 768, 768], P('section', 'tensor')
- feedforward_fresh: bfloat16 [2, 3072, 768], P('section', 'tensor')
- gain_momentum_new: float32 [2, 768], P('section', 'tensor')
- gain_weight_new: float32 [2, 768], P('section', 'tensor')
- bias_momentum_new: float32 [12, 32], P('tensor')
- bias_weight_new: float32 [12, 32], P('tensor')
The draws below stay inside these ranges and needn't reach their ends.
All inputs are finite; a program needn't handle non-finite values.
Results may differ from the reference program's by a relative error of at most 0.0004.
Values may be sent and summed in bfloat16 or wider, within the bound.
A program may use at most 64 MiB of HBM per device.

```python
import math
import jax
import jax.numpy as jnp
from jax import lax

D = 768
FF = 3072
HEADS = 12
BUCKETS = 32
RANK = 32
NS_STEPS = 5
REPLICAS = 16


def scaled_field(key, replica_count, matrix_count, row_count, col_count):
    keys = jax.random.split(key, 3)
    full_shape = (replica_count, matrix_count, row_count, col_count)
    rising = 0.5 * jnp.exp(math.log(3.0) * jnp.arange(row_count, dtype=jnp.float32) / row_count)
    row_scale = rising.reshape(1, 1, row_count, 1) * jnp.exp(jax.random.uniform(keys[1], (1, matrix_count, row_count, 1), jnp.float32, math.log(0.4), math.log(2.5)))
    col_scale = jnp.exp(jax.random.uniform(keys[2], (1, matrix_count, 1, col_count), jnp.float32, math.log(0.33), math.log(3.0)))
    values = jax.random.truncated_normal(keys[0], -4.0, 4.0, full_shape, jnp.float32)
    return values * row_scale * col_scale


def draw_attention_grads(key, part):
    return scaled_field(jax.random.fold_in(key, 11), REPLICAS, 4, D, D)


def draw_feedforward_grads(key, part):
    return scaled_field(jax.random.fold_in(key, 23), REPLICAS, 2, FF, D)


def steps_of(key, dims, pieces, least, largest):
    def one(axis_at, blocks):
        heights = jax.random.uniform(jax.random.fold_in(jax.random.fold_in(key, 6), axis_at), (blocks,), jnp.float32, least / len(pieces), largest / len(pieces))
        return jnp.repeat(jnp.exp(heights), dims[axis_at] // blocks).reshape((-1,) + (1,) * (len(dims) - axis_at - 1))

    level = one(*pieces[0])
    for cut in pieces[1:]:
        level = level * one(*cut)
    return level


def normal_values(own_key, extent, width, most, pieces=(), kind=jnp.bfloat16):
    values = width * jax.random.normal(own_key, extent, jnp.float32)
    if pieces:
        values = values * steps_of(own_key, extent, pieces, -0.22, 0.18)
    return jnp.clip(values, -most, most).astype(kind)


def setup_inputs(seed: int = 0) -> dict:
    streams_of = jax.random.split(jax.random.key(seed), 17)
    return {
        "attention_grads": draw_attention_grads(jax.random.fold_in(streams_of[16], 71), 0),
        "feedforward_grads": draw_feedforward_grads(jax.random.fold_in(streams_of[16], 71), 0),
        "attention_errors": normal_values(streams_of[2], (REPLICAS, 4, D, D), 0.5, 3.0, ((0, 16), (1, 2), (2, 4)), jnp.float32),
        "feedforward_errors": normal_values(streams_of[3], (REPLICAS, 2, FF, D), 0.5, 3.0, ((0, 16), (1, 2), (2, 4)), jnp.float32),
        "attention_factor": normal_values(streams_of[4], (4, D, RANK), D ** -0.5, 0.21875, ((0, 2),), jnp.float32),
        "feedforward_factor": normal_values(streams_of[5], (2, D, RANK), D ** -0.5, 0.21875, ((0, 2),), jnp.float32),
        "attention_momentum": normal_values(streams_of[6], (4, D, D), 0.5, 3.0, ((0, 2), (1, 4), (2, 16)), jnp.float32),
        "feedforward_momentum": normal_values(streams_of[7], (2, FF, D), 0.5, 3.0, ((0, 2), (1, 4), (2, 16)), jnp.float32),
        "attention_master": normal_values(streams_of[8], (4, D, D), 0.5, 3.0, ((0, 2), (1, 4), (2, 16)), jnp.float32),
        "feedforward_master": normal_values(streams_of[9], (2, FF, D), 0.5, 3.0, ((0, 2), (1, 4), (2, 16)), jnp.float32),
        "gain_grads": normal_values(streams_of[10], (REPLICAS, 2, D), 1.0, 6.0, ((0, 16), (1, 2), (2, 4)), jnp.float32),
        "bias_grads": normal_values(streams_of[11], (REPLICAS, HEADS, BUCKETS), 1.0, 6.0, ((0, 16), (1, 4)), jnp.float32),
        "gain_momentum": normal_values(streams_of[12], (2, D), 0.5, 3.0, ((0, 2), (1, 4)), jnp.float32),
        "gain_weight": jnp.clip(1.0 + 0.1 * jax.random.normal(streams_of[13], (2, D), jnp.float32), 0.5, 1.5),
        "bias_momentum": normal_values(streams_of[14], (HEADS, BUCKETS), 0.5, 3.0, ((0, 4),), jnp.float32),
        "bias_weight": normal_values(streams_of[15], (HEADS, BUCKETS), 1.0, 4.0, ((0, 4),), jnp.float32),
    }


exact_mode = lax.Precision.HIGHEST
learn_rate = 0.05
decay_rate = 0.9

def inverse_root(gram_matrix):
    identity = jnp.broadcast_to(jnp.eye(gram_matrix.shape[-1], dtype=jnp.float32), gram_matrix.shape)
    frob_scale = jnp.sqrt(lax.optimization_barrier(jnp.sum(gram_matrix * gram_matrix, axis=(-2, -1), keepdims=True))) + 1e-06
    converge = gram_matrix / frob_scale
    inverse = identity
    for turn_index in range(NS_STEPS):
        middle = 0.5 * (3.0 * identity - jnp.matmul(inverse, converge, precision=exact_mode))
        converge, inverse = (jnp.matmul(converge, middle, precision=exact_mode), jnp.matmul(middle, inverse, precision=exact_mode))
    return inverse / jnp.sqrt(frob_scale)

def compress(grads, errors, factor, momentum, master):
    merged = grads + errors
    power = jnp.einsum('rmij,mjk->mik', merged, factor, precision=exact_mode)
    gram_power = jnp.einsum('mik,mil->mkl', power, power, precision=exact_mode)
    ortho = jnp.matmul(power, inverse_root(gram_power), precision=exact_mode)
    back = jnp.einsum('rmij,mik->mjk', merged, ortho, precision=exact_mode) / REPLICAS
    approx = jnp.einsum('mik,mjk->mij', ortho, back, precision=exact_mode)
    errors_new = merged - approx[None]
    gram_back = jnp.einsum('mjk,mjl->mkl', back, back, precision=exact_mode)
    factor_new = jnp.matmul(back, inverse_root(gram_back), precision=exact_mode)
    momentum_new = decay_rate * momentum + approx
    base = master - learn_rate * decay_rate * momentum
    master_new = base - learn_rate * approx
    fresh = master_new.astype(jnp.bfloat16)
    return (errors_new, factor_new, momentum_new, master_new, fresh)

def reference(attention_grads, feedforward_grads, attention_errors, feedforward_errors, attention_factor, feedforward_factor, attention_momentum, feedforward_momentum, attention_master, feedforward_master, gain_grads, bias_grads, gain_momentum, gain_weight, bias_momentum, bias_weight):
    attn_out = compress(attention_grads, attention_errors, attention_factor, attention_momentum, attention_master)
    feed_out = compress(feedforward_grads, feedforward_errors, feedforward_factor, feedforward_momentum, feedforward_master)
    gain_momentum_new = decay_rate * gain_momentum + lax.optimization_barrier(jnp.sum(gain_grads, axis=0)) / REPLICAS
    gain_weight_new = gain_weight - learn_rate * gain_momentum_new
    bias_momentum_new = decay_rate * bias_momentum + lax.optimization_barrier(jnp.sum(bias_grads, axis=0)) / REPLICAS
    bias_weight_new = bias_weight - learn_rate * bias_momentum_new
    return (attn_out[0], feed_out[0], attn_out[1], feed_out[1], attn_out[2], feed_out[2], attn_out[3], feed_out[3], attn_out[4], feed_out[4], gain_momentum_new, gain_weight_new, bias_momentum_new, bias_weight_new)
```

```python
import jax
import jax.numpy as jnp
from jax import lax
from jax.experimental import pallas as pl
from jax.experimental.pallas import tpu as pltpu
from jax.sharding import PartitionSpec as P

NS_STEPS = 5
RANK = 32
MESH = pl.DeviceIdType.MESH

exact_mode = lax.Precision.HIGHEST
learn_rate = 0.05
decay_rate = 0.9


def dot(a, b, dims):
    return lax.dot_general(
        a, b, ((dims[:1], dims[1:]), ((), ())), precision=exact_mode,
        preferred_element_type=jnp.float32,
    )


def block_mask(size):
    row = lax.broadcasted_iota(jnp.int32, (size, size), 0)
    col = lax.broadcasted_iota(jnp.int32, (size, size), 1)
    return (row >> 5) == (col >> 5), row == col


def inverse_root(gram):
    size = gram.shape[0]
    _, diagonal = block_mask(size)
    identity = jnp.where(diagonal, 1.0, 0.0).astype(jnp.float32)
    squares = jnp.sum(gram * gram, axis=1, keepdims=True)
    scale = jnp.concatenate(
        [
            jnp.broadcast_to(
                jnp.sqrt(jnp.sum(squares[at : at + RANK], axis=0, keepdims=True)) + 1e-06,
                (RANK, 1),
            )
            for at in range(0, size, RANK)
        ],
        axis=0,
    )
    converge = gram / scale
    inverse = None
    for turn in range(NS_STEPS):
        product = converge if turn == 0 else dot(inverse, converge, (1, 0))
        middle = 0.5 * (3.0 * identity - product)
        inverse = middle if turn == 0 else dot(middle, inverse, (1, 0))
        if turn < NS_STEPS - 1:
            converge = dot(converge, middle, (1, 0))
    return inverse / jnp.sqrt(scale)


def remote(src, dst, send_sem, recv_sem, device):
    return pltpu.make_async_remote_copy(
        src_ref=src, dst_ref=dst, send_sem=send_sem, recv_sem=recv_sem,
        device_id=device, device_id_type=MESH,
    )


CHUNKS = 12


def exchange_kernel(
    att_grads, ff_grads, att_errors, ff_errors, factor, base, small,
    ortho_out, back_out, factor_out, small_out, base_out,
    merged, errors, part, part_slots, power, gram_slots, back_part, back_slots,
    back_pieces, back, small_slots,
    load_sem, base_sem, part_send, part_recv, power_send, power_recv, gram_send, gram_recv,
    bpart_send, bpart_recv, piece_send, piece_recv, back_send, back_recv,
    small_send, small_recv, first_send, first_recv, second_send, second_recv,
):
    me = lax.axis_index("shard")
    my_tensor = lax.axis_index("tensor")
    my_y, my_z = me // 4, me % 4
    rows = (384, 768)

    def shard_peer(d):
        return lax.rem(me + d, 16)

    def shard_source(d):
        return lax.rem(me + 16 - d, 16)

    loads = []
    for at, (g, e) in enumerate(((att_grads, att_errors), (ff_grads, ff_errors))):
        for piece in range(1 if at == 0 else 2):
            source = pl.ds(piece * 384, 384)
            target = pl.ds((at + piece) * 384, 384)
            n = at + piece
            loads.append((
                pltpu.make_async_copy(g.at[source], merged.at[target], load_sem.at[n, 0]),
                pltpu.make_async_copy(e.at[source], errors.at[target], load_sem.at[n, 1]),
            ))
    for g, e in loads:
        g.start()
        e.start()
    own_base = pltpu.make_async_copy(base, base_out.at[my_y, my_z], base_sem)
    own_base.start()

    barrier = pltpu.get_barrier_semaphore()

    @pl.loop(1, 16)
    def _(d):
        pl.semaphore_signal(barrier, inc=1, device_id={"shard": shard_peer(d)}, device_id_type=MESH)

    for d in range(1, 4):
        pl.semaphore_signal(
            barrier, inc=1, device_id={"tensor": lax.rem(my_tensor + d, 4)}, device_id_type=MESH
        )

    lane = lax.broadcasted_iota(jnp.int32, (RANK, 384), 1)
    for n in range(3):
        for copy in loads[n]:
            copy.wait()
        at = pl.ds(n * 384, 384)
        total = merged[at] + errors[at]
        merged[at] = total
        if n == 0:
            both = dot(total, factor[0:64], (1, 1)).T
            left = jnp.where(lane < 192, both[0:32], both[32:64])
        else:
            left = dot(total, factor[64:96], (1, 1)).T
        part[4 * n : 4 * n + 4] = left.reshape(4, 8, 384)
    small_slots[me] = small[...]

    pl.semaphore_wait(barrier, 18)

    def part_copy(d):
        return remote(
            part.at[lax.rem(shard_peer(d), CHUNKS)], part_slots.at[d], part_send.at[d],
            part_recv.at[d], {"shard": shard_peer(d)},
        )

    def small_copy(d):
        return remote(
            small_slots.at[me], small_slots.at[me], small_send.at[d], small_recv.at[d],
            {"shard": shard_peer(d)},
        )

    @pl.loop(1, 16)
    def _(d):
        @pl.when(shard_peer(d) < CHUNKS)
        def _():
            part_copy(d).start()

    def first_copy(half, d):
        if half == 0:
            device = {"shard": lax.rem(my_y + d, 4) * 4 + my_z}
        else:
            device = {"shard": my_y * 4 + lax.rem(my_z + d, 4)}
        return remote(
            base.at[half], base_out.at[my_y, my_z, half], first_send.at[half, d],
            first_recv.at[half, d], device,
        )

    def second_copy(half, d):
        if half == 0:
            device = {"shard": my_y * 4 + lax.rem(my_z + d, 4)}
            piece = base_out.at[:, my_z, 0]
        else:
            device = {"shard": lax.rem(my_y + d, 4) * 4 + my_z}
            piece = base_out.at[my_y, :, 1]
        return remote(piece, piece, second_send.at[half, d], second_recv.at[half, d], device)

    for half in range(2):
        for d in range(1, 4):
            first_copy(half, d).start()

    @pl.loop(1, 16)
    def _(d):
        small_copy(d).start()

    def power_copy(d):
        return remote(
            power.at[me], power.at[me], power_send.at[d], power_recv.at[d],
            {"shard": shard_peer(d)},
        )

    @pl.when(me < CHUNKS)
    def _():
        @pl.loop(1, 16)
        def _(d):
            part_copy(d).wait_recv()

        total = part[me]
        for d in range(1, 16):
            total += part_slots[d]
        power[me] = total

        @pl.loop(1, 16)
        def _(d):
            power_copy(d).start()

    own_base.wait()
    for half in range(2):
        for d in range(1, 4):
            first_copy(half, d).wait_recv()
    for half in range(2):
        for d in range(1, 4):
            second_copy(half, d).start()

    @pl.loop(1, 16)
    def _(d):
        @pl.when(shard_source(d) < CHUNKS)
        def _():
            remote(
                power.at[0], power.at[0], power_send.at[d], power_recv.at[d],
                {"shard": shard_peer(d)},
            ).wait_recv()

    zeros = jnp.zeros((RANK, 384), jnp.float32)
    spread = []
    for n in range(3):
        left = power[4 * n : 4 * n + 4].reshape(RANK, 384)
        if n == 0:
            spread.append(
                jnp.concatenate(
                    [jnp.where(lane < 192, left, 0.0), jnp.where(lane < 192, 0.0, left), zeros], axis=0
                )
            )
        else:
            spread.append(jnp.concatenate([zeros, zeros, left], axis=0))
    blocks, _ = block_mask(96)
    gram = dot(spread[0], spread[0], (1, 1))
    gram += dot(spread[1], spread[1], (1, 1))
    gram += dot(spread[2], spread[2], (1, 1))
    gram_slots[my_tensor] = gram[0:32] + gram[32:64] + gram[64:96]

    def gram_copy(d):
        return remote(
            gram_slots.at[my_tensor], gram_slots.at[my_tensor], gram_send.at[d], gram_recv.at[d],
            {"tensor": lax.rem(my_tensor + d, 4)},
        )

    for d in range(1, 4):
        gram_copy(d).start()
    for d in range(1, 4):
        gram_copy(d).wait_recv()
    total = (gram_slots[0] + gram_slots[1]) + (gram_slots[2] + gram_slots[3])
    root = inverse_root(jnp.where(blocks, jnp.concatenate([total, total, total], axis=0), 0.0))

    right = None
    for n in range(3):
        ortho = dot(root, spread[n], (0, 0))
        ortho_out[:, n * 384 : n * 384 + 384] = ortho
        term = dot(ortho, merged[n * 384 : n * 384 + 384], (1, 0))
        right = term if right is None else right + term
    back_part[...] = right.reshape(CHUNKS, 8, 768)

    def bpart_copy(d):
        return remote(
            back_part.at[lax.rem(shard_peer(d), CHUNKS)], back_slots.at[d], bpart_send.at[d],
            bpart_recv.at[d], {"shard": shard_peer(d)},
        )

    def piece_copy(d):
        return remote(
            back_pieces.at[my_tensor], back_pieces.at[my_tensor], piece_send.at[d],
            piece_recv.at[d], {"tensor": lax.rem(my_tensor + d, 4)},
        )

    def back_copy(d):
        return remote(
            back.at[me], back.at[me], back_send.at[d], back_recv.at[d],
            {"shard": shard_peer(d)},
        )

    @pl.loop(1, 16)
    def _(d):
        @pl.when(shard_peer(d) < CHUNKS)
        def _():
            bpart_copy(d).start()

    @pl.when(me < CHUNKS)
    def _():
        @pl.loop(1, 16)
        def _(d):
            bpart_copy(d).wait_recv()

        total = back_part[me]
        for d in range(1, 16):
            total += back_slots[d]
        back_pieces[my_tensor] = total
        for d in range(1, 4):
            piece_copy(d).start()
        for d in range(1, 4):
            piece_copy(d).wait_recv()
        total = (back_pieces[0] + back_pieces[1]) + (back_pieces[2] + back_pieces[3])
        back[me] = total * (1.0 / 16.0)

        @pl.loop(1, 16)
        def _(d):
            back_copy(d).start()

    @pl.loop(1, 16)
    def _(d):
        @pl.when(shard_source(d) < CHUNKS)
        def _():
            remote(
                back.at[0], back.at[0], back_send.at[d], back_recv.at[d],
                {"shard": shard_peer(d)},
            ).wait_recv()

    total = back[...].reshape(96, 768)
    back_out[...] = total
    root = inverse_root(jnp.where(blocks, dot(total, total, (1, 1)), 0.0))
    factor_out[...] = dot(root, total, (0, 0))

    @pl.loop(1, 16)
    def _(d):
        small_copy(d).wait_recv()

    total = small_slots[0]
    for n in range(1, 16):
        total += small_slots[n]
    small_out[...] = total

    for half in range(2):
        for d in range(1, 4):
            second_copy(half, d).wait_recv()

    @pl.loop(1, 16)
    def _(d):
        small_copy(d).wait_send()

        @pl.when(shard_peer(d) < CHUNKS)
        def _():
            part_copy(d).wait_send()
            bpart_copy(d).wait_send()

    @pl.when(me < CHUNKS)
    def _():
        @pl.loop(1, 16)
        def _(d):
            power_copy(d).wait_send()
            back_copy(d).wait_send()

        for d in range(1, 4):
            piece_copy(d).wait_send()

    for d in range(1, 4):
        gram_copy(d).wait_send()
        for half in range(2):
            first_copy(half, d).wait_send()
            second_copy(half, d).wait_send()


def exchange(att_grads, ff_grads, att_errors, ff_errors, factor, base, small):
    any_spec = pl.BlockSpec(memory_space=pl.ANY)
    vmem_spec = pl.BlockSpec(memory_space=pltpu.VMEM)
    dma = pltpu.SemaphoreType.DMA
    f32 = jnp.float32
    return pl.pallas_call(
        exchange_kernel,
        out_shape=(
            jax.ShapeDtypeStruct((96, 1152), f32),
            jax.ShapeDtypeStruct((96, 768), f32),
            jax.ShapeDtypeStruct((96, 768), f32),
            jax.ShapeDtypeStruct((8, 128), f32),
            jax.ShapeDtypeStruct((4, 4, 2, 24, 1152), f32),
        ),
        in_specs=[any_spec] * 4 + [vmem_spec] * 3,
        out_specs=(vmem_spec, vmem_spec, vmem_spec, vmem_spec, any_spec),
        scratch_shapes=[
            pltpu.VMEM((1152, 768), f32),
            pltpu.VMEM((1152, 768), f32),
            pltpu.VMEM((12, 8, 384), f32),
            pltpu.VMEM((16, 8, 384), f32),
            pltpu.VMEM((12, 8, 384), f32),
            pltpu.VMEM((4, 32, 96), f32),
            pltpu.VMEM((12, 8, 768), f32),
            pltpu.VMEM((16, 8, 768), f32),
            pltpu.VMEM((4, 8, 768), f32),
            pltpu.VMEM((12, 8, 768), f32),
            pltpu.VMEM((16, 8, 128), f32),
            dma((3, 2)),
            dma,
        ]
        + [dma((16,))] * 4
        + [dma((4,))] * 2
        + [dma((16,))] * 2
        + [dma((4,))] * 2
        + [dma((16,))] * 4
        + [dma((2, 4))] * 4,
        compiler_params=pltpu.CompilerParams(
            collective_id=0, has_side_effects=True, vmem_limit_bytes=40 * 1024 * 1024
        ),
        name="exchange",
    )(att_grads, ff_grads, att_errors, ff_errors, factor, base, small)


def per_device(
    attention_grads,
    feedforward_grads,
    attention_errors,
    feedforward_errors,
    attention_factor,
    feedforward_factor,
    attention_momentum,
    feedforward_momentum,
    attention_master,
    feedforward_master,
    gain_grads,
    bias_grads,
    gain_momentum,
    gain_weight,
    bias_momentum,
    bias_weight,
):
    replicas = 16
    start = lax.axis_index("shard") * 48
    att_grads = attention_grads.reshape(384, 768)
    ff_grads = feedforward_grads.reshape(768, 768)
    att_errors = attention_errors.reshape(384, 768)
    ff_errors = feedforward_errors.reshape(768, 768)
    factor = jnp.concatenate([attention_factor, feedforward_factor], axis=0)
    factor = jnp.swapaxes(factor, 1, 2).reshape(96, 768)

    def columns(att, ff):
        return jnp.concatenate([att[0].T, att[1].T, ff[0].T], axis=1)

    momentum = columns(attention_momentum, feedforward_momentum)
    master = columns(attention_master, feedforward_master)
    base = master - learn_rate * decay_rate * momentum
    small = jnp.concatenate([gain_grads.reshape(2, 96), bias_grads.reshape(1, 96)], axis=0)
    small = jnp.pad(small, ((0, 5), (0, 32)))
    ortho, back, factor_new, small_total, base_full = exchange(
        att_grads, ff_grads, att_errors, ff_errors, factor, base.reshape(2, 24, 1152), small
    )

    approx = dot(ortho, back, (0, 0))
    att_errors_new = att_grads + att_errors - approx[:384]
    ff_errors_new = ff_grads + ff_errors - approx[384:]
    own = dot(lax.dynamic_slice_in_dim(back, start, 48, 1), ortho, (0, 0))
    momentum_new = decay_rate * momentum + own
    master_new = base - learn_rate * own
    fresh = base_full.reshape(768, 1152).T - learn_rate * approx
    fresh = fresh.astype(jnp.bfloat16)

    def split(values):
        return (
            jnp.stack([values[:, :192].T, values[:, 192:384].T]),
            values[:, 384:].T[None],
        )

    att_momentum_new, ff_momentum_new = split(momentum_new)
    att_master_new, ff_master_new = split(master_new)
    factor_new = jnp.swapaxes(factor_new.reshape(3, 32, 768), 1, 2)
    gain_total = small_total[0:2, :96].reshape(1, 192)
    bias_total = small_total[2:3, :96].reshape(3, 32)
    gain_momentum_new = decay_rate * gain_momentum + gain_total / replicas
    gain_weight_new = gain_weight - learn_rate * gain_momentum_new
    bias_momentum_new = decay_rate * bias_momentum + bias_total / replicas
    bias_weight_new = bias_weight - learn_rate * bias_momentum_new
    return (
        att_errors_new.reshape(1, 2, 192, 768),
        ff_errors_new.reshape(1, 1, 768, 768),
        factor_new[:2],
        factor_new[2:],
        att_momentum_new,
        ff_momentum_new,
        att_master_new,
        ff_master_new,
        fresh[:384].reshape(2, 192, 768),
        fresh[384:].reshape(1, 768, 768),
        gain_momentum_new,
        gain_weight_new,
        bias_momentum_new,
        bias_weight_new,
    )


def solution(mesh):
    placed = (
        P("shard", "section", "tensor", None),
        P("shard", "section", "tensor", None),
        P("shard", "section", "tensor", None),
        P("shard", "section", "tensor", None),
        P("section", None, None),
        P("section", None, None),
        P("section", "tensor", "shard"),
        P("section", "tensor", "shard"),
        P("section", "tensor", "shard"),
        P("section", "tensor", "shard"),
        P("shard", "section", "tensor"),
        P("shard", "tensor", None),
        P("section", "tensor"),
        P("section", "tensor"),
        P("tensor", None),
        P("tensor", None),
    )
    return jax.shard_map(
        per_device,
        mesh=mesh,
        in_specs=placed,
        out_specs=(
            P("shard", "section", "tensor", None),
            P("shard", "section", "tensor", None),
            P("section", None, None),
            P("section", None, None),
            P("section", "tensor", "shard"),
            P("section", "tensor", "shard"),
            P("section", "tensor", "shard"),
            P("section", "tensor", "shard"),
            P("section", "tensor", None),
            P("section", "tensor", None),
            P("section", "tensor"),
            P("section", "tensor"),
            P("tensor", None),
            P("tensor", None),
        ),
        check_vma=False,
    )
```

```python
import jax
import jax.numpy as jnp
from jax import lax
from jax.experimental import pallas as pl
from jax.experimental.pallas import tpu as pltpu
from jax.sharding import PartitionSpec as P

NS_STEPS = 5
RANK = 32
MESH = pl.DeviceIdType.MESH

exact_mode = lax.Precision.HIGHEST
learn_rate = 0.05
decay_rate = 0.9


def dot(a, b, dims):
    return lax.dot_general(
        a, b, ((dims[:1], dims[1:]), ((), ())), precision=exact_mode,
        preferred_element_type=jnp.float32,
    )


def block_mask(size):
    row = lax.broadcasted_iota(jnp.int32, (size, size), 0)
    col = lax.broadcasted_iota(jnp.int32, (size, size), 1)
    return (row >> 5) == (col >> 5), row == col


def inverse_root(gram):
    size = gram.shape[0]
    _, diagonal = block_mask(size)
    identity = jnp.where(diagonal, 1.0, 0.0).astype(jnp.float32)
    squares = jnp.sum(gram * gram, axis=1, keepdims=True)
    scale = jnp.concatenate(
        [
            jnp.broadcast_to(
                jnp.sqrt(jnp.sum(squares[at : at + RANK], axis=0, keepdims=True)) + 1e-06,
                (RANK, 1),
            )
            for at in range(0, size, RANK)
        ],
        axis=0,
    )
    converge = gram / scale
    inverse = None
    for turn in range(NS_STEPS):
        product = converge if turn == 0 else dot(inverse, converge, (1, 0))
        middle = 0.5 * (3.0 * identity - product)
        inverse = middle if turn == 0 else dot(middle, inverse, (1, 0))
        if turn < NS_STEPS - 1:
            converge = dot(converge, middle, (1, 0))
    return inverse / jnp.sqrt(scale)


def remote(src, dst, send_sem, recv_sem, device):
    return pltpu.make_async_remote_copy(
        src_ref=src, dst_ref=dst, send_sem=send_sem, recv_sem=recv_sem,
        device_id=device, device_id_type=MESH,
    )


CHUNKS = 12


def exchange_kernel(
    att_grads, ff_grads, att_errors, ff_errors, att_factor_in, ff_factor_in,
    att_momentum_in, ff_momentum_in, att_master_in, ff_master_in, gain, bias,
    ortho_out, back_out, factor_out, small_out, base_out,
    merged, errors, factor, att_momentum, ff_momentum, att_master, ff_master, base, part, part_slots, power, gram_slots, back_part, back_slots,
    back_pieces, back, small_slots,
    load_sem, state_sem, base_sem, part_send, part_recv, power_send, power_recv, gram_send, gram_recv,
    bpart_send, bpart_recv, piece_send, piece_recv, back_send, back_recv,
    small_send, small_recv, first_send, first_recv, second_send, second_recv,
):
    me = lax.axis_index("shard")
    my_tensor = lax.axis_index("tensor")
    my_y, my_z = me // 4, me % 4
    rows = (384, 768)

    def shard_peer(d):
        return lax.rem(me + d, 16)

    def shard_source(d):
        return lax.rem(me + 16 - d, 16)

    loads = []
    for at, (g, e) in enumerate(((att_grads, att_errors), (ff_grads, ff_errors))):
        for piece in range(1 if at == 0 else 2):
            source = pl.ds(piece * 384, 384)
            target = pl.ds((at + piece) * 384, 384)
            n = at + piece
            loads.append((
                pltpu.make_async_copy(g.at[source], merged.at[target], load_sem.at[n, 0]),
                pltpu.make_async_copy(e.at[source], errors.at[target], load_sem.at[n, 1]),
            ))
    states = [
        pltpu.make_async_copy(source, target, state_sem.at[n])
        for n, (source, target) in enumerate((
            (att_momentum_in, att_momentum), (ff_momentum_in, ff_momentum),
            (att_master_in, att_master), (ff_master_in, ff_master),
            (att_factor_in, factor.at[pl.ds(0, 64)]), (ff_factor_in, factor.at[pl.ds(64, 32)]),
        ))
    ]
    for copy in states:
        copy.start()
    for g, e in loads:
        g.start()
        e.start()

    barrier = pltpu.get_barrier_semaphore()

    @pl.loop(1, 16)
    def _(d):
        pl.semaphore_signal(barrier, inc=1, device_id={"shard": shard_peer(d)}, device_id_type=MESH)

    for d in range(1, 4):
        pl.semaphore_signal(
            barrier, inc=1, device_id={"tensor": lax.rem(my_tensor + d, 4)}, device_id_type=MESH
        )

    def part_copy(d):
        return remote(
            part.at[lax.rem(shard_peer(d), CHUNKS)], part_slots.at[d], part_send.at[d],
            part_recv.at[d], {"shard": shard_peer(d)},
        )

    def small_copy(d):
        return remote(
            small_slots.at[me], small_slots.at[me], small_send.at[d], small_recv.at[d],
            {"shard": shard_peer(d)},
        )

    def first_copy(half, d):
        if half == 0:
            device = {"shard": lax.rem(my_y + d, 4) * 4 + my_z}
        else:
            device = {"shard": my_y * 4 + lax.rem(my_z + d, 4)}
        return remote(
            base.at[half], base_out.at[my_y, my_z, half], first_send.at[half, d],
            first_recv.at[half, d], device,
        )

    def second_copy(half, d):
        if half == 0:
            device = {"shard": my_y * 4 + lax.rem(my_z + d, 4)}
            piece = base_out.at[:, my_z, 0]
        else:
            device = {"shard": lax.rem(my_y + d, 4) * 4 + my_z}
            piece = base_out.at[my_y, :, 1]
        return remote(piece, piece, second_send.at[half, d], second_recv.at[half, d], device)

    for copy in states:
        copy.wait()
    step = learn_rate * decay_rate
    for half in range(2):
        at = slice(24 * half, 24 * half + 24)
        att = att_master[:, at] - step * att_momentum[:, at]
        base[half, :, 0:384] = jnp.concatenate([att[0], att[1]], axis=1)
        base[half, :, 384:1152] = ff_master[at] - step * ff_momentum[at]
    own_base = pltpu.make_async_copy(base, base_out.at[my_y, my_z], base_sem)
    own_base.start()
    small_slots[me, 0:1, 0:192] = gain[...]
    small_slots[me, 1:4, 0:32] = bias[...]

    lane = lax.broadcasted_iota(jnp.int32, (RANK, 384), 1)
    for n in range(3):
        for copy in loads[n]:
            copy.wait()
        at = pl.ds(n * 384, 384)
        total = merged[at] + errors[at]
        merged[at] = total
        if n == 0:
            both = dot(total, factor[0:64], (1, 1)).T
            left = jnp.where(lane < 192, both[0:32], both[32:64])
        else:
            left = dot(total, factor[64:96], (1, 1)).T
        part[4 * n : 4 * n + 4] = left.reshape(4, 8, 384)
        if n == 0:
            pl.semaphore_wait(barrier, 18)

        @pl.loop(1, 16)
        def _(d):
            @pl.when((shard_peer(d) >= 4 * n) & (shard_peer(d) < 4 * n + 4))
            def _():
                part_copy(d).start()

        if n == 0:
            for half in range(2):
                for d in range(1, 4):
                    first_copy(half, d).start()

    @pl.loop(1, 16)
    def _(d):
        small_copy(d).start()

    def power_copy(d):
        return remote(
            power.at[me], power.at[me], power_send.at[d], power_recv.at[d],
            {"shard": shard_peer(d)},
        )

    @pl.when(me < CHUNKS)
    def _():
        @pl.loop(1, 16)
        def _(d):
            part_copy(d).wait_recv()

        total = part[me]
        for d in range(1, 16):
            total += part_slots[d]
        power[me] = total

        @pl.loop(1, 16)
        def _(d):
            power_copy(d).start()

    own_base.wait()
    for half in range(2):
        for d in range(1, 4):
            first_copy(half, d).wait_recv()
    for half in range(2):
        for d in range(1, 4):
            second_copy(half, d).start()

    @pl.loop(1, 16)
    def _(d):
        @pl.when(shard_source(d) < CHUNKS)
        def _():
            remote(
                power.at[0], power.at[0], power_send.at[d], power_recv.at[d],
                {"shard": shard_peer(d)},
            ).wait_recv()

    zeros = jnp.zeros((RANK, 384), jnp.float32)
    spread = []
    for n in range(3):
        left = power[4 * n : 4 * n + 4].reshape(RANK, 384)
        if n == 0:
            spread.append(
                jnp.concatenate(
                    [jnp.where(lane < 192, left, 0.0), jnp.where(lane < 192, 0.0, left), zeros], axis=0
                )
            )
        else:
            spread.append(jnp.concatenate([zeros, zeros, left], axis=0))
    blocks, _ = block_mask(96)
    gram = dot(spread[0], spread[0], (1, 1))
    gram += dot(spread[1], spread[1], (1, 1))
    gram += dot(spread[2], spread[2], (1, 1))
    gram_slots[my_tensor] = gram[0:32] + gram[32:64] + gram[64:96]

    def gram_copy(d):
        return remote(
            gram_slots.at[my_tensor], gram_slots.at[my_tensor], gram_send.at[d], gram_recv.at[d],
            {"tensor": lax.rem(my_tensor + d, 4)},
        )

    for d in range(1, 4):
        gram_copy(d).start()
    for d in range(1, 4):
        gram_copy(d).wait_recv()
    total = (gram_slots[0] + gram_slots[1]) + (gram_slots[2] + gram_slots[3])
    root = inverse_root(jnp.where(blocks, jnp.concatenate([total, total, total], axis=0), 0.0))

    right = None
    for n in range(3):
        ortho = dot(root, spread[n], (0, 0))
        ortho_out[:, n * 384 : n * 384 + 384] = ortho
        term = dot(ortho, merged[n * 384 : n * 384 + 384], (1, 0))
        right = term if right is None else right + term
    back_part[...] = right.reshape(CHUNKS, 8, 768)

    def bpart_copy(d):
        return remote(
            back_part.at[lax.rem(shard_peer(d), CHUNKS)], back_slots.at[d], bpart_send.at[d],
            bpart_recv.at[d], {"shard": shard_peer(d)},
        )

    def piece_copy(d):
        return remote(
            back_pieces.at[my_tensor], back_pieces.at[my_tensor], piece_send.at[d],
            piece_recv.at[d], {"tensor": lax.rem(my_tensor + d, 4)},
        )

    def back_copy(d):
        return remote(
            back.at[me], back.at[me], back_send.at[d], back_recv.at[d],
            {"shard": shard_peer(d)},
        )

    @pl.loop(1, 16)
    def _(d):
        @pl.when(shard_peer(d) < CHUNKS)
        def _():
            bpart_copy(d).start()

    @pl.when(me < CHUNKS)
    def _():
        @pl.loop(1, 16)
        def _(d):
            bpart_copy(d).wait_recv()

        total = back_part[me]
        for d in range(1, 16):
            total += back_slots[d]
        back_pieces[my_tensor] = total
        for d in range(1, 4):
            piece_copy(d).start()
        for d in range(1, 4):
            piece_copy(d).wait_recv()
        total = (back_pieces[0] + back_pieces[1]) + (back_pieces[2] + back_pieces[3])
        back[me] = total * (1.0 / 16.0)

        @pl.loop(1, 16)
        def _(d):
            back_copy(d).start()

    @pl.loop(1, 16)
    def _(d):
        @pl.when(shard_source(d) < CHUNKS)
        def _():
            remote(
                back.at[0], back.at[0], back_send.at[d], back_recv.at[d],
                {"shard": shard_peer(d)},
            ).wait_recv()

    total = back[...].reshape(96, 768)
    back_out[...] = total
    root = inverse_root(jnp.where(blocks, dot(total, total, (1, 1)), 0.0))
    factor_out[...] = dot(root, total, (0, 0))

    @pl.loop(1, 16)
    def _(d):
        small_copy(d).wait_recv()

    total = small_slots[0]
    for n in range(1, 16):
        total += small_slots[n]
    small_out[...] = total

    for half in range(2):
        for d in range(1, 4):
            second_copy(half, d).wait_recv()

    @pl.loop(1, 16)
    def _(d):
        small_copy(d).wait_send()

        @pl.when(shard_peer(d) < CHUNKS)
        def _():
            part_copy(d).wait_send()
            bpart_copy(d).wait_send()

    @pl.when(me < CHUNKS)
    def _():
        @pl.loop(1, 16)
        def _(d):
            power_copy(d).wait_send()
            back_copy(d).wait_send()

        for d in range(1, 4):
            piece_copy(d).wait_send()

    for d in range(1, 4):
        gram_copy(d).wait_send()
        for half in range(2):
            first_copy(half, d).wait_send()
            second_copy(half, d).wait_send()


def exchange(*operands):
    any_spec = pl.BlockSpec(memory_space=pl.ANY)
    vmem_spec = pl.BlockSpec(memory_space=pltpu.VMEM)
    dma = pltpu.SemaphoreType.DMA
    f32 = jnp.float32
    return pl.pallas_call(
        exchange_kernel,
        out_shape=(
            jax.ShapeDtypeStruct((96, 1152), f32),
            jax.ShapeDtypeStruct((96, 768), f32),
            jax.ShapeDtypeStruct((96, 768), f32),
            jax.ShapeDtypeStruct((8, 256), f32),
            jax.ShapeDtypeStruct((4, 4, 2, 24, 1152), f32),
        ),
        in_specs=[any_spec] * 10 + [vmem_spec] * 2,
        out_specs=(vmem_spec, vmem_spec, vmem_spec, vmem_spec, any_spec),
        scratch_shapes=[
            pltpu.VMEM((1152, 768), f32),
            pltpu.VMEM((1152, 768), f32),
            pltpu.VMEM((96, 768), f32),
            pltpu.VMEM((2, 48, 192), f32),
            pltpu.VMEM((48, 768), f32),
            pltpu.VMEM((2, 48, 192), f32),
            pltpu.VMEM((48, 768), f32),
            pltpu.VMEM((2, 24, 1152), f32),
            pltpu.VMEM((12, 8, 384), f32),
            pltpu.VMEM((16, 8, 384), f32),
            pltpu.VMEM((12, 8, 384), f32),
            pltpu.VMEM((4, 32, 96), f32),
            pltpu.VMEM((12, 8, 768), f32),
            pltpu.VMEM((16, 8, 768), f32),
            pltpu.VMEM((4, 8, 768), f32),
            pltpu.VMEM((12, 8, 768), f32),
            pltpu.VMEM((16, 8, 256), f32),
            dma((3, 2)),
            dma((6,)),
            dma,
        ]
        + [dma((16,))] * 4
        + [dma((4,))] * 2
        + [dma((16,))] * 2
        + [dma((4,))] * 2
        + [dma((16,))] * 4
        + [dma((2, 4))] * 4,
        compiler_params=pltpu.CompilerParams(collective_id=0, has_side_effects=True),
        name="exchange",
    )(*operands)


ROWS = 128


def update_kernel(
    att_grads, att_errors, ff_grads, ff_errors, ortho, back, base,
    att_momentum, ff_momentum, att_master, ff_master, small,
    gain_momentum, gain_weight, bias_momentum, bias_weight,
    att_errors_out, ff_errors_out, att_fresh_out, ff_fresh_out,
    att_momentum_out, ff_momentum_out, att_master_out, ff_master_out,
    gain_momentum_out, gain_weight_out, bias_momentum_out, bias_weight_out,
):
    n = pl.program_id(0)
    at = pl.ds(pl.multiple_of(n * ROWS, ROWS), ROWS)
    approx = dot(ortho[:, at], back[...], (0, 0))
    fresh = (base[...].T - learn_rate * approx).astype(jnp.bfloat16)

    @pl.when(n < 3)
    def _():
        att_errors_out[...] = att_grads[...] + att_errors[...] - approx
        att_fresh_out[...] = fresh

    @pl.when(n >= 3)
    def _():
        ff_errors_out[...] = ff_grads[...] + ff_errors[...] - approx
        ff_fresh_out[...] = fresh

    @pl.when(n == 0)
    def _():
        shard = lax.axis_index("shard")
        own_back = pltpu.roll(back[...], lax.rem(768 - 48 * shard, 768), 1)[:, 0:128]
        own = dot(own_back, ortho[...], (0, 0))[0:48]
        step = learn_rate * decay_rate
        att_own = own[:, 0:384]
        for m in range(2):
            piece = (att_own if m == 0 else pltpu.roll(att_own, 192, 1))[:, 0:192]
            att_momentum_out[m] = decay_rate * att_momentum[m] + piece
            att_master_out[m] = att_master[m] - step * att_momentum[m] - learn_rate * piece
        piece = own[:, 384:1152]
        ff_momentum_out[...] = decay_rate * ff_momentum[...] + piece
        ff_master_out[...] = ff_master[...] - step * ff_momentum[...] - learn_rate * piece
        gain = decay_rate * gain_momentum[...] + small[0:1, 0:192] * (1.0 / 16.0)
        gain_momentum_out[...] = gain
        gain_weight_out[...] = gain_weight[...] - learn_rate * gain
        bias = decay_rate * bias_momentum[...] + small[1:4, 0:32] * (1.0 / 16.0)
        bias_momentum_out[...] = bias
        bias_weight_out[...] = bias_weight[...] - learn_rate * bias


def update(*operands):
    def att_block(n):
        return jnp.minimum(n, 2), 0

    def ff_block(n):
        return jnp.maximum(n - 3, 0), 0

    def whole(*shape):
        return pl.BlockSpec(shape, lambda n: (0,) * len(shape))

    att = pl.BlockSpec((ROWS, 768), att_block)
    ff = pl.BlockSpec((ROWS, 768), ff_block)
    states = [whole(2, 48, 192), whole(48, 768)]
    vectors = [whole(1, 192)] * 2 + [whole(3, 32)] * 2
    shapes = [
        ((384, 768), jnp.float32), ((768, 768), jnp.float32),
        ((384, 768), jnp.bfloat16), ((768, 768), jnp.bfloat16),
        ((2, 48, 192), jnp.float32), ((48, 768), jnp.float32),
        ((2, 48, 192), jnp.float32), ((48, 768), jnp.float32),
        ((1, 192), jnp.float32), ((1, 192), jnp.float32),
        ((3, 32), jnp.float32), ((3, 32), jnp.float32),
    ]
    return pl.pallas_call(
        update_kernel,
        grid=(1152 // ROWS,),
        out_shape=[jax.ShapeDtypeStruct(*shape) for shape in shapes],
        in_specs=[att, att, ff, ff, whole(96, 1152), whole(96, 768)]
        + [pl.BlockSpec((768, ROWS), lambda n: (0, n))]
        + states + states + [whole(8, 256)] + vectors,
        out_specs=[att, ff, att, ff] + states + states + vectors,
        name="update",
    )(*operands)


def per_device(
    attention_grads,
    feedforward_grads,
    attention_errors,
    feedforward_errors,
    attention_factor,
    feedforward_factor,
    attention_momentum,
    feedforward_momentum,
    attention_master,
    feedforward_master,
    gain_grads,
    bias_grads,
    gain_momentum,
    gain_weight,
    bias_momentum,
    bias_weight,
):
    att_grads = attention_grads.reshape(384, 768)
    ff_grads = feedforward_grads.reshape(768, 768)
    att_errors = attention_errors.reshape(384, 768)
    ff_errors = feedforward_errors.reshape(768, 768)
    states = (
        jnp.swapaxes(attention_momentum, 1, 2), feedforward_momentum[0].T,
        jnp.swapaxes(attention_master, 1, 2), feedforward_master[0].T,
    )
    ortho, back, factor_new, small_total, base_full = exchange(
        att_grads, ff_grads, att_errors, ff_errors,
        jnp.swapaxes(attention_factor, 1, 2).reshape(64, 768), feedforward_factor[0].T,
        *states, gain_grads.reshape(1, 192), bias_grads.reshape(3, 32),
    )
    (
        att_errors_new, ff_errors_new, att_fresh, ff_fresh,
        att_momentum_new, ff_momentum_new, att_master_new, ff_master_new, *vectors,
    ) = update(
        att_grads, att_errors, ff_grads, ff_errors, ortho, back, base_full.reshape(768, 1152),
        *states, small_total, gain_momentum, gain_weight, bias_momentum, bias_weight,
    )
    factor_new = jnp.swapaxes(factor_new.reshape(3, 32, 768), 1, 2)
    return (
        att_errors_new.reshape(1, 2, 192, 768),
        ff_errors_new.reshape(1, 1, 768, 768),
        factor_new[:2],
        factor_new[2:],
        jnp.swapaxes(att_momentum_new, 1, 2),
        ff_momentum_new.T[None],
        jnp.swapaxes(att_master_new, 1, 2),
        ff_master_new.T[None],
        att_fresh.reshape(2, 192, 768),
        ff_fresh.reshape(1, 768, 768),
        *vectors,
    )


def solution(mesh):
    placed = (
        P("shard", "section", "tensor", None),
        P("shard", "section", "tensor", None),
        P("shard", "section", "tensor", None),
        P("shard", "section", "tensor", None),
        P("section", None, None),
        P("section", None, None),
        P("section", "tensor", "shard"),
        P("section", "tensor", "shard"),
        P("section", "tensor", "shard"),
        P("section", "tensor", "shard"),
        P("shard", "section", "tensor"),
        P("shard", "tensor", None),
        P("section", "tensor"),
        P("section", "tensor"),
        P("tensor", None),
        P("tensor", None),
    )
    return jax.shard_map(
        per_device,
        mesh=mesh,
        in_specs=placed,
        out_specs=(
            P("shard", "section", "tensor", None),
            P("shard", "section", "tensor", None),
            P("section", None, None),
            P("section", None, None),
            P("section", "tensor", "shard"),
            P("section", "tensor", "shard"),
            P("section", "tensor", "shard"),
            P("section", "tensor", "shard"),
            P("section", "tensor", None),
            P("section", "tensor", None),
            P("section", "tensor"),
            P("section", "tensor"),
            P("tensor", None),
            P("tensor", None),
        ),
        check_vma=False,
    )
```

```python
import jax
import jax.numpy as jnp
from jax import lax
from jax.experimental import pallas as pl
from jax.experimental.pallas import tpu as pltpu
from jax.sharding import PartitionSpec as P

NS_STEPS = 5
RANK = 32
MESH = pl.DeviceIdType.MESH

exact_mode = lax.Precision.HIGHEST
learn_rate = 0.05
decay_rate = 0.9


def dot(a, b, dims):
    return lax.dot_general(
        a, b, ((dims[:1], dims[1:]), ((), ())), precision=exact_mode,
        preferred_element_type=jnp.float32,
    )


def halves(value):
    high = value.astype(jnp.bfloat16)
    return high, (value - high.astype(jnp.float32)).astype(jnp.bfloat16)


def short_dot(a, b, dims):
    return lax.dot_general(
        a, b, ((dims[:1], dims[1:]), ((), ())), preferred_element_type=jnp.float32
    )


def block_mask(size):
    row = lax.broadcasted_iota(jnp.int32, (size, size), 0)
    col = lax.broadcasted_iota(jnp.int32, (size, size), 1)
    return (row >> 5) == (col >> 5), row == col


def inverse_root(gram):
    size = gram.shape[0]
    _, diagonal = block_mask(size)
    identity = jnp.where(diagonal, 1.0, 0.0).astype(jnp.float32)
    squares = jnp.sum(gram * gram, axis=1, keepdims=True)
    scale = jnp.concatenate(
        [
            jnp.broadcast_to(
                jnp.sqrt(jnp.sum(squares[at : at + RANK], axis=0, keepdims=True)) + 1e-06,
                (RANK, 1),
            )
            for at in range(0, size, RANK)
        ],
        axis=0,
    )
    converge = gram / scale
    inverse = None
    for turn in range(NS_STEPS):
        product = converge if turn == 0 else dot(inverse, converge, (1, 0))
        middle = 0.5 * (3.0 * identity - product)
        inverse = middle if turn == 0 else dot(middle, inverse, (1, 0))
        if turn < NS_STEPS - 1:
            converge = dot(converge, middle, (1, 0))
    return inverse / jnp.sqrt(scale)


def remote(src, dst, send_sem, recv_sem, device):
    return pltpu.make_async_remote_copy(
        src_ref=src, dst_ref=dst, send_sem=send_sem, recv_sem=recv_sem,
        device_id=device, device_id_type=MESH,
    )


CHUNKS = 12


def exchange_kernel(
    att_grads, ff_grads, att_errors, ff_errors, att_factor_in, ff_factor_in,
    att_momentum_in, ff_momentum_in, att_master_in, ff_master_in, gain, bias,
    ortho_out, back_out, factor_out, small_out, base_out,
    merged, errors, merged_high, merged_low, factor, att_momentum, ff_momentum, att_master, ff_master, base, part, part_slots, power, gram_slots, back_part, back_slots,
    back_pieces, back, small_slots,
    load_sem, state_sem, base_sem, part_send, part_recv, power_send, power_recv, gram_send, gram_recv,
    bpart_send, bpart_recv, piece_send, piece_recv, back_send, back_recv,
    small_send, small_recv, first_send, first_recv, second_send, second_recv,
):
    me = lax.axis_index("shard")
    my_tensor = lax.axis_index("tensor")
    my_y, my_z = me // 4, me % 4
    rows = (384, 768)

    def shard_peer(d):
        return lax.rem(me + d, 16)

    def shard_source(d):
        return lax.rem(me + 16 - d, 16)

    loads = []
    for at, (g, e) in enumerate(((att_grads, att_errors), (ff_grads, ff_errors))):
        for piece in range(1 if at == 0 else 2):
            source = pl.ds(piece * 384, 384)
            target = pl.ds((at + piece) * 384, 384)
            n = at + piece
            loads.append((
                pltpu.make_async_copy(g.at[source], merged.at[target], load_sem.at[n, 0]),
                pltpu.make_async_copy(e.at[source], errors.at[target], load_sem.at[n, 1]),
            ))
    states = [
        pltpu.make_async_copy(source, target, state_sem.at[n])
        for n, (source, target) in enumerate((
            (att_momentum_in, att_momentum), (ff_momentum_in, ff_momentum),
            (att_master_in, att_master), (ff_master_in, ff_master),
            (att_factor_in, factor.at[pl.ds(0, 64)]), (ff_factor_in, factor.at[pl.ds(64, 32)]),
        ))
    ]
    for copy in states:
        copy.start()
    for g, e in loads:
        g.start()
        e.start()

    barrier = pltpu.get_barrier_semaphore()

    @pl.loop(1, 16)
    def _(d):
        pl.semaphore_signal(barrier, inc=1, device_id={"shard": shard_peer(d)}, device_id_type=MESH)

    for d in range(1, 4):
        pl.semaphore_signal(
            barrier, inc=1, device_id={"tensor": lax.rem(my_tensor + d, 4)}, device_id_type=MESH
        )

    def part_copy(d):
        return remote(
            part.at[lax.rem(shard_peer(d), CHUNKS)], part_slots.at[d], part_send.at[d],
            part_recv.at[d], {"shard": shard_peer(d)},
        )

    def small_copy(d):
        return remote(
            small_slots.at[me], small_slots.at[me], small_send.at[d], small_recv.at[d],
            {"shard": shard_peer(d)},
        )

    def first_copy(half, d):
        if half == 0:
            device = {"shard": lax.rem(my_y + d, 4) * 4 + my_z}
        else:
            device = {"shard": my_y * 4 + lax.rem(my_z + d, 4)}
        return remote(
            base.at[half], base_out.at[my_y, my_z, half], first_send.at[half, d],
            first_recv.at[half, d], device,
        )

    def second_copy(half, d):
        if half == 0:
            device = {"shard": my_y * 4 + lax.rem(my_z + d, 4)}
            piece = base_out.at[:, my_z, 0]
        else:
            device = {"shard": lax.rem(my_y + d, 4) * 4 + my_z}
            piece = base_out.at[my_y, :, 1]
        return remote(piece, piece, second_send.at[half, d], second_recv.at[half, d], device)

    for copy in states:
        copy.wait()
    step = learn_rate * decay_rate
    for half in range(2):
        at = slice(24 * half, 24 * half + 24)
        att = att_master[:, at] - step * att_momentum[:, at]
        base[half, :, 0:384] = jnp.concatenate([att[0], att[1]], axis=1)
        base[half, :, 384:1152] = ff_master[at] - step * ff_momentum[at]
    own_base = pltpu.make_async_copy(base, base_out.at[my_y, my_z], base_sem)
    own_base.start()
    small_slots[me, 0:1, 0:192] = gain[...]
    small_slots[me, 1:4, 0:32] = bias[...].reshape(3, 32)

    lane = lax.broadcasted_iota(jnp.int32, (RANK, 384), 1)
    for n in range(3):
        for copy in loads[n]:
            copy.wait()
        at = pl.ds(n * 384, 384)
        high, low = halves(merged[at] + errors[at])
        merged_high[at] = high
        merged_low[at] = low
        if n == 0:
            size, (factor_high, factor_low) = 64, halves(factor[0:64])
        else:
            size, (factor_high, factor_low) = 32, halves(factor[64:96])
        both = short_dot(high, jnp.concatenate([factor_high, factor_low], axis=0), (1, 1))
        left = (both[:, 0:size] + both[:, size : 2 * size] + short_dot(low, factor_high, (1, 1))).T
        if n == 0:
            left = jnp.where(lane < 192, left[0:32], left[32:64])
        part[4 * n : 4 * n + 4] = left.reshape(4, 8, 384)
        if n == 0:
            pl.semaphore_wait(barrier, 18)

        @pl.loop(1, 16)
        def _(d):
            @pl.when((shard_peer(d) >= 4 * n) & (shard_peer(d) < 4 * n + 4))
            def _():
                part_copy(d).start()

        if n == 0:
            for half in range(2):
                for d in range(1, 4):
                    first_copy(half, d).start()

    @pl.loop(1, 16)
    def _(d):
        small_copy(d).start()

    def power_copy(d):
        return remote(
            power.at[me], power.at[me], power_send.at[d], power_recv.at[d],
            {"shard": shard_peer(d)},
        )

    @pl.when(me < CHUNKS)
    def _():
        @pl.loop(1, 16)
        def _(d):
            part_copy(d).wait_recv()

        total = part[me]
        for d in range(1, 16):
            total += part_slots[d]
        power[me] = total

        @pl.loop(1, 16)
        def _(d):
            power_copy(d).start()

    own_base.wait()
    for half in range(2):
        for d in range(1, 4):
            first_copy(half, d).wait_recv()
    for half in range(2):
        for d in range(1, 4):
            second_copy(half, d).start()

    @pl.loop(1, 16)
    def _(d):
        @pl.when(shard_source(d) < CHUNKS)
        def _():
            remote(
                power.at[0], power.at[0], power_send.at[d], power_recv.at[d],
                {"shard": shard_peer(d)},
            ).wait_recv()

    zeros = jnp.zeros((RANK, 384), jnp.float32)
    spread = []
    for n in range(3):
        left = power[4 * n : 4 * n + 4].reshape(RANK, 384)
        if n == 0:
            spread.append(
                jnp.concatenate(
                    [jnp.where(lane < 192, left, 0.0), jnp.where(lane < 192, 0.0, left), zeros], axis=0
                )
            )
        else:
            spread.append(jnp.concatenate([zeros, zeros, left], axis=0))
    blocks, _ = block_mask(96)
    gram = dot(spread[0], spread[0], (1, 1))
    gram += dot(spread[1], spread[1], (1, 1))
    gram += dot(spread[2], spread[2], (1, 1))
    gram_slots[my_tensor] = gram[0:32] + gram[32:64] + gram[64:96]

    def gram_copy(d):
        return remote(
            gram_slots.at[my_tensor], gram_slots.at[my_tensor], gram_send.at[d], gram_recv.at[d],
            {"tensor": lax.rem(my_tensor + d, 4)},
        )

    for d in range(1, 4):
        gram_copy(d).start()
    for d in range(1, 4):
        gram_copy(d).wait_recv()
    total = (gram_slots[0] + gram_slots[1]) + (gram_slots[2] + gram_slots[3])
    root = inverse_root(jnp.where(blocks, jnp.concatenate([total, total, total], axis=0), 0.0))

    terms = []
    for n in range(3):
        at = slice(n * 384, n * 384 + 384)
        used = slice(0, 64) if n == 0 else slice(64, 96)
        ortho = dot(root, spread[n], (0, 0))
        ortho_out[:, at] = ortho
        ortho_high, ortho_low = halves(ortho[used])
        size = 64 if n == 0 else 32
        both = short_dot(jnp.concatenate([ortho_high, ortho_low], axis=0), merged_high[at], (1, 0))
        terms.append(
            both[0:size] + both[size : 2 * size] + short_dot(ortho_high, merged_low[at], (1, 0))
        )
    back_part[0:8] = terms[0].reshape(8, 8, 768)
    back_part[8:12] = (terms[1] + terms[2]).reshape(4, 8, 768)

    def bpart_copy(d):
        return remote(
            back_part.at[lax.rem(shard_peer(d), CHUNKS)], back_slots.at[d], bpart_send.at[d],
            bpart_recv.at[d], {"shard": shard_peer(d)},
        )

    def piece_copy(d):
        return remote(
            back_pieces.at[my_tensor], back_pieces.at[my_tensor], piece_send.at[d],
            piece_recv.at[d], {"tensor": lax.rem(my_tensor + d, 4)},
        )

    def back_copy(d):
        return remote(
            back.at[me], back.at[me], back_send.at[d], back_recv.at[d],
            {"shard": shard_peer(d)},
        )

    @pl.loop(1, 16)
    def _(d):
        @pl.when(shard_peer(d) < CHUNKS)
        def _():
            bpart_copy(d).start()

    @pl.when(me < CHUNKS)
    def _():
        @pl.loop(1, 16)
        def _(d):
            bpart_copy(d).wait_recv()

        total = back_part[me]
        for d in range(1, 16):
            total += back_slots[d]
        back_pieces[my_tensor] = total
        for d in range(1, 4):
            piece_copy(d).start()
        for d in range(1, 4):
            piece_copy(d).wait_recv()
        total = (back_pieces[0] + back_pieces[1]) + (back_pieces[2] + back_pieces[3])
        back[me] = total * (1.0 / 16.0)

        @pl.loop(1, 16)
        def _(d):
            back_copy(d).start()

    @pl.loop(1, 16)
    def _(d):
        @pl.when(shard_source(d) < CHUNKS)
        def _():
            remote(
                back.at[0], back.at[0], back_send.at[d], back_recv.at[d],
                {"shard": shard_peer(d)},
            ).wait_recv()

    total = back[...].reshape(96, 768)
    back_out[...] = total
    root = inverse_root(jnp.where(blocks, dot(total, total, (1, 1)), 0.0))
    factor_out[...] = dot(root, total, (0, 0))

    @pl.loop(1, 16)
    def _(d):
        small_copy(d).wait_recv()

    total = small_slots[0]
    for n in range(1, 16):
        total += small_slots[n]
    small_out[...] = total

    for half in range(2):
        for d in range(1, 4):
            second_copy(half, d).wait_recv()

    @pl.loop(1, 16)
    def _(d):
        small_copy(d).wait_send()

        @pl.when(shard_peer(d) < CHUNKS)
        def _():
            part_copy(d).wait_send()
            bpart_copy(d).wait_send()

    @pl.when(me < CHUNKS)
    def _():
        @pl.loop(1, 16)
        def _(d):
            power_copy(d).wait_send()
            back_copy(d).wait_send()

        for d in range(1, 4):
            piece_copy(d).wait_send()

    for d in range(1, 4):
        gram_copy(d).wait_send()
        for half in range(2):
            first_copy(half, d).wait_send()
            second_copy(half, d).wait_send()


def exchange(*operands):
    any_spec = pl.BlockSpec(memory_space=pl.ANY)
    vmem_spec = pl.BlockSpec(memory_space=pltpu.VMEM)
    dma = pltpu.SemaphoreType.DMA
    f32 = jnp.float32
    return pl.pallas_call(
        exchange_kernel,
        out_shape=(
            jax.ShapeDtypeStruct((96, 1152), f32),
            jax.ShapeDtypeStruct((96, 768), f32),
            jax.ShapeDtypeStruct((96, 768), f32),
            jax.ShapeDtypeStruct((8, 256), f32),
            jax.ShapeDtypeStruct((4, 4, 2, 24, 1152), f32),
        ),
        in_specs=[any_spec] * 10 + [vmem_spec] * 2,
        out_specs=(vmem_spec, vmem_spec, vmem_spec, vmem_spec, any_spec),
        scratch_shapes=[
            pltpu.VMEM((1152, 768), f32),
            pltpu.VMEM((1152, 768), f32),
            pltpu.VMEM((1152, 768), jnp.bfloat16),
            pltpu.VMEM((1152, 768), jnp.bfloat16),
            pltpu.VMEM((96, 768), f32),
            pltpu.VMEM((2, 48, 192), f32),
            pltpu.VMEM((48, 768), f32),
            pltpu.VMEM((2, 48, 192), f32),
            pltpu.VMEM((48, 768), f32),
            pltpu.VMEM((2, 24, 1152), f32),
            pltpu.VMEM((12, 8, 384), f32),
            pltpu.VMEM((16, 8, 384), f32),
            pltpu.VMEM((12, 8, 384), f32),
            pltpu.VMEM((4, 32, 96), f32),
            pltpu.VMEM((12, 8, 768), f32),
            pltpu.VMEM((16, 8, 768), f32),
            pltpu.VMEM((4, 8, 768), f32),
            pltpu.VMEM((12, 8, 768), f32),
            pltpu.VMEM((16, 8, 256), f32),
            dma((3, 2)),
            dma((6,)),
            dma,
        ]
        + [dma((16,))] * 4
        + [dma((4,))] * 2
        + [dma((16,))] * 2
        + [dma((4,))] * 2
        + [dma((16,))] * 4
        + [dma((2, 4))] * 4,
        compiler_params=pltpu.CompilerParams(collective_id=0, has_side_effects=True),
        name="exchange",
    )(*operands)


ROWS = 128


def update_kernel(
    att_grads, att_errors, ff_grads, ff_errors, ortho, back, base,
    att_momentum, ff_momentum, att_master, ff_master, small, factor,
    gain_momentum, gain_weight, bias_momentum, bias_weight,
    att_errors_out, ff_errors_out, att_fresh_out, ff_fresh_out,
    att_momentum_out, ff_momentum_out, att_master_out, ff_master_out,
    gain_momentum_out, gain_weight_out, bias_momentum_out, bias_weight_out,
    att_factor_out, ff_factor_out,
):
    n = pl.program_id(0)
    at = pl.ds(pl.multiple_of(n * ROWS, ROWS), ROWS)

    def product(used):
        left_high, left_low = halves(ortho[used, at])
        right_high, right_low = halves(back[used])
        return short_dot(
            jnp.concatenate([left_high, left_high, left_low], axis=0),
            jnp.concatenate([right_high, right_low, right_high], axis=0),
            (0, 0),
        )

    @pl.when(n < 3)
    def _():
        approx = product(slice(0, 64))
        fresh = (base[...].T - learn_rate * approx).astype(jnp.bfloat16)
        att_errors_out[...] = att_grads[...] + att_errors[...] - approx
        att_fresh_out[...] = fresh

    @pl.when(n >= 3)
    def _():
        approx = product(slice(64, 96))
        fresh = (base[...].T - learn_rate * approx).astype(jnp.bfloat16)
        ff_errors_out[...] = ff_grads[...] + ff_errors[...] - approx
        ff_fresh_out[...] = fresh

    @pl.when(n == 0)
    def _():
        shard = lax.axis_index("shard")
        own_back = pltpu.roll(back[...], lax.rem(768 - 48 * shard, 768), 1)[:, 0:128]
        own = dot(own_back, ortho[...], (0, 0))[0:48]
        step = learn_rate * decay_rate
        att_own = own[:, 0:384]
        for m in range(2):
            piece = (att_own if m == 0 else pltpu.roll(att_own, 192, 1))[:, 0:192]
            att_momentum_out[m] = decay_rate * att_momentum[m] + piece
            att_master_out[m] = att_master[m] - step * att_momentum[m] - learn_rate * piece
        piece = own[:, 384:1152]
        ff_momentum_out[...] = decay_rate * ff_momentum[...] + piece
        ff_master_out[...] = ff_master[...] - step * ff_momentum[...] - learn_rate * piece
        gain = decay_rate * gain_momentum[...] + small[0:1, 0:192] * (1.0 / 16.0)
        gain_momentum_out[...] = gain
        gain_weight_out[...] = gain_weight[...] - learn_rate * gain
        bias = decay_rate * bias_momentum[...] + small[1:4, 0:32] * (1.0 / 16.0)
        bias_momentum_out[...] = bias
        bias_weight_out[...] = bias_weight[...] - learn_rate * bias
        att_factor_out[...] = factor[0:64]
        ff_factor_out[...] = factor[64:96]


def update(*operands):
    def att_block(n):
        return jnp.minimum(n, 2), 0

    def ff_block(n):
        return jnp.maximum(n - 3, 0), 0

    def whole(*shape):
        return pl.BlockSpec(shape, lambda n: (0,) * len(shape))

    att = pl.BlockSpec((ROWS, 768), att_block)
    ff = pl.BlockSpec((ROWS, 768), ff_block)
    states = [whole(2, 48, 192), whole(48, 768)]
    vectors = [whole(1, 192)] * 2 + [whole(3, 32)] * 2
    shapes = [
        ((384, 768), jnp.float32), ((768, 768), jnp.float32),
        ((384, 768), jnp.bfloat16), ((768, 768), jnp.bfloat16),
        ((2, 48, 192), jnp.float32), ((48, 768), jnp.float32),
        ((2, 48, 192), jnp.float32), ((48, 768), jnp.float32),
        ((1, 192), jnp.float32), ((1, 192), jnp.float32),
        ((3, 32), jnp.float32), ((3, 32), jnp.float32),
        ((64, 768), jnp.float32), ((32, 768), jnp.float32),
    ]
    return pl.pallas_call(
        update_kernel,
        grid=(1152 // ROWS,),
        out_shape=[jax.ShapeDtypeStruct(*shape) for shape in shapes],
        in_specs=[att, att, ff, ff, whole(96, 1152), whole(96, 768)]
        + [pl.BlockSpec((768, ROWS), lambda n: (0, n))]
        + states + states + [whole(8, 256), whole(96, 768)] + vectors,
        out_specs=[att, ff, att, ff] + states + states + vectors
        + [whole(64, 768), whole(32, 768)],
        name="update",
    )(*operands)


def per_device(
    attention_grads,
    feedforward_grads,
    attention_errors,
    feedforward_errors,
    attention_factor,
    feedforward_factor,
    attention_momentum,
    feedforward_momentum,
    attention_master,
    feedforward_master,
    gain_grads,
    bias_grads,
    gain_momentum,
    gain_weight,
    bias_momentum,
    bias_weight,
):
    att_grads = attention_grads.reshape(384, 768)
    ff_grads = feedforward_grads.reshape(768, 768)
    att_errors = attention_errors.reshape(384, 768)
    ff_errors = feedforward_errors.reshape(768, 768)
    states = (
        jnp.swapaxes(attention_momentum, 1, 2), feedforward_momentum[0].T,
        jnp.swapaxes(attention_master, 1, 2), feedforward_master[0].T,
    )
    ortho, back, factor_new, small_total, base_full = exchange(
        att_grads, ff_grads, att_errors, ff_errors,
        jnp.swapaxes(attention_factor, 1, 2).reshape(64, 768), feedforward_factor[0].T,
        *states, gain_grads.reshape(1, 192), jnp.swapaxes(bias_grads, 0, 1),
    )
    (
        att_errors_new, ff_errors_new, att_fresh, ff_fresh,
        att_momentum_new, ff_momentum_new, att_master_new, ff_master_new, *vectors,
        att_factor_new, ff_factor_new,
    ) = update(
        att_grads, att_errors, ff_grads, ff_errors, ortho, back, base_full.reshape(768, 1152),
        *states, small_total, factor_new, gain_momentum, gain_weight, bias_momentum, bias_weight,
    )
    return (
        att_errors_new.reshape(1, 2, 192, 768),
        ff_errors_new.reshape(1, 1, 768, 768),
        jnp.swapaxes(att_factor_new.reshape(2, 32, 768), 1, 2),
        ff_factor_new.T[None],
        jnp.swapaxes(att_momentum_new, 1, 2),
        ff_momentum_new.T[None],
        jnp.swapaxes(att_master_new, 1, 2),
        ff_master_new.T[None],
        att_fresh.reshape(2, 192, 768),
        ff_fresh.reshape(1, 768, 768),
        *vectors,
    )


def solution(mesh):
    placed = (
        P("shard", "section", "tensor", None),
        P("shard", "section", "tensor", None),
        P("shard", "section", "tensor", None),
        P("shard", "section", "tensor", None),
        P("section", None, None),
        P("section", None, None),
        P("section", "tensor", "shard"),
        P("section", "tensor", "shard"),
        P("section", "tensor", "shard"),
        P("section", "tensor", "shard"),
        P("shard", "section", "tensor"),
        P("shard", "tensor", None),
        P("section", "tensor"),
        P("section", "tensor"),
        P("tensor", None),
        P("tensor", None),
    )
    return jax.shard_map(
        per_device,
        mesh=mesh,
        in_specs=placed,
        out_specs=(
            P("shard", "section", "tensor", None),
            P("shard", "section", "tensor", None),
            P("section", None, None),
            P("section", None, None),
            P("section", "tensor", "shard"),
            P("section", "tensor", "shard"),
            P("section", "tensor", "shard"),
            P("section", "tensor", "shard"),
            P("section", "tensor", None),
            P("section", "tensor", None),
            P("section", "tensor"),
            P("section", "tensor"),
            P("tensor", None),
            P("tensor", None),
        ),
        check_vma=False,
    )
```

```python
import jax
import jax.numpy as jnp
from jax import lax
from jax.experimental import pallas as pl
from jax.experimental.pallas import tpu as pltpu
from jax.sharding import PartitionSpec as P

NS_STEPS = 5
RANK = 32
MESH = pl.DeviceIdType.MESH

exact_mode = lax.Precision.HIGHEST
learn_rate = 0.05
decay_rate = 0.9


def dot(a, b, dims):
    return lax.dot_general(
        a, b, ((dims[:1], dims[1:]), ((), ())), precision=exact_mode,
        preferred_element_type=jnp.float32,
    )


def halves(value):
    high = value.astype(jnp.bfloat16)
    return high, (value - high.astype(jnp.float32)).astype(jnp.bfloat16)


def short_dot(a, b, dims):
    return lax.dot_general(
        a, b, ((dims[:1], dims[1:]), ((), ())), preferred_element_type=jnp.float32
    )


def block_mask(size):
    row = lax.broadcasted_iota(jnp.int32, (size, size), 0)
    col = lax.broadcasted_iota(jnp.int32, (size, size), 1)
    return (row >> 5) == (col >> 5), row == col


def inverse_root(gram):
    size = gram.shape[0]
    _, diagonal = block_mask(size)
    identity = jnp.where(diagonal, 1.0, 0.0).astype(jnp.float32)
    squares = jnp.sum(gram * gram, axis=1, keepdims=True)
    scale = jnp.concatenate(
        [
            jnp.broadcast_to(
                jnp.sqrt(jnp.sum(squares[at : at + RANK], axis=0, keepdims=True)) + 1e-06,
                (RANK, 1),
            )
            for at in range(0, size, RANK)
        ],
        axis=0,
    )
    converge = gram / scale
    inverse = None
    for turn in range(NS_STEPS):
        product = converge if turn == 0 else dot(inverse, converge, (1, 0))
        middle = 0.5 * (3.0 * identity - product)
        inverse = middle if turn == 0 else dot(middle, inverse, (1, 0))
        if turn < NS_STEPS - 1:
            converge = dot(converge, middle, (1, 0))
    return inverse / jnp.sqrt(scale)


def remote(src, dst, send_sem, recv_sem, device):
    return pltpu.make_async_remote_copy(
        src_ref=src, dst_ref=dst, send_sem=send_sem, recv_sem=recv_sem,
        device_id=device, device_id_type=MESH,
    )


CHUNKS = 12


def exchange_kernel(
    att_grads, ff_grads, att_errors, ff_errors, att_factor_in, ff_factor_in,
    att_momentum_in, ff_momentum_in, att_master_in, ff_master_in, gain, bias,
    ortho_out, back_out, factor_out, small_out, base_out,
    merged, errors, merged_high, merged_low, factor, att_momentum, ff_momentum, att_master, ff_master, base, part, part_slots, power, gram_slots, back_part, back_slots,
    back_pieces, back, small_slots,
    load_sem, state_sem, base_sem, part_send, part_recv, power_send, power_recv, gram_send, gram_recv,
    bpart_send, bpart_recv, piece_send, piece_recv, back_send, back_recv,
    small_send, small_recv, first_send, first_recv, second_send, second_recv,
):
    me = lax.axis_index("shard")
    my_tensor = lax.axis_index("tensor")
    my_y, my_z = me // 4, me % 4
    rows = (384, 768)

    def shard_peer(d):
        return lax.rem(me + d, 16)

    def shard_source(d):
        return lax.rem(me + 16 - d, 16)

    loads = []
    for at, (g, e) in enumerate(((att_grads, att_errors), (ff_grads, ff_errors))):
        for piece in range(1 if at == 0 else 2):
            source = pl.ds(piece * 384, 384)
            target = pl.ds((at + piece) * 384, 384)
            n = at + piece
            loads.append((
                pltpu.make_async_copy(g.at[source], merged.at[target], load_sem.at[n, 0]),
                pltpu.make_async_copy(e.at[source], errors.at[target], load_sem.at[n, 1]),
            ))
    states = [
        pltpu.make_async_copy(source, target, state_sem.at[n])
        for n, (source, target) in enumerate((
            (att_momentum_in, att_momentum), (ff_momentum_in, ff_momentum),
            (att_master_in, att_master), (ff_master_in, ff_master),
            (att_factor_in, factor.at[pl.ds(0, 64)]), (ff_factor_in, factor.at[pl.ds(64, 32)]),
        ))
    ]
    for copy in states:
        copy.start()
    for g, e in loads:
        g.start()
        e.start()

    barrier = pltpu.get_barrier_semaphore()

    @pl.loop(1, 16)
    def _(d):
        pl.semaphore_signal(barrier, inc=1, device_id={"shard": shard_peer(d)}, device_id_type=MESH)

    for d in range(1, 4):
        pl.semaphore_signal(
            barrier, inc=1, device_id={"tensor": lax.rem(my_tensor + d, 4)}, device_id_type=MESH
        )

    def part_copy(d):
        return remote(
            part.at[lax.rem(shard_peer(d), CHUNKS)], part_slots.at[d], part_send.at[d],
            part_recv.at[d], {"shard": shard_peer(d)},
        )

    def small_copy(d):
        return remote(
            small_slots.at[me], small_slots.at[me], small_send.at[d], small_recv.at[d],
            {"shard": shard_peer(d)},
        )

    def first_copy(half, d):
        if half == 0:
            device = {"shard": lax.rem(my_y + d, 4) * 4 + my_z}
        else:
            device = {"shard": my_y * 4 + lax.rem(my_z + d, 4)}
        return remote(
            base.at[half], base_out.at[my_y, my_z, half], first_send.at[half, d],
            first_recv.at[half, d], device,
        )

    def second_copy(half, d):
        if half == 0:
            device = {"shard": my_y * 4 + lax.rem(my_z + d, 4)}
            piece = base_out.at[:, my_z, 0]
        else:
            device = {"shard": lax.rem(my_y + d, 4) * 4 + my_z}
            piece = base_out.at[my_y, :, 1]
        return remote(piece, piece, second_send.at[half, d], second_recv.at[half, d], device)

    for copy in states:
        copy.wait()
    step = learn_rate * decay_rate
    for half in range(2):
        at = slice(24 * half, 24 * half + 24)
        att = att_master[:, at] - step * att_momentum[:, at]
        base[half, :, 0:384] = jnp.concatenate([att[0], att[1]], axis=1)
        base[half, :, 384:1152] = ff_master[at] - step * ff_momentum[at]
    own_base = pltpu.make_async_copy(base, base_out.at[my_y, my_z], base_sem)
    own_base.start()
    small_slots[me, 0:1, 0:192] = gain[...]
    small_slots[me, 1:4, 0:32] = bias[...].reshape(3, 32)

    lane = lax.broadcasted_iota(jnp.int32, (RANK, 384), 1)
    for n in range(3):
        for copy in loads[n]:
            copy.wait()
        at = pl.ds(n * 384, 384)
        high, low = halves(merged[at] + errors[at])
        merged_high[at] = high
        merged_low[at] = low
        if n == 0:
            size, (factor_high, factor_low) = 64, halves(factor[0:64])
        else:
            size, (factor_high, factor_low) = 32, halves(factor[64:96])
        both = short_dot(high, jnp.concatenate([factor_high, factor_low], axis=0), (1, 1))
        left = (both[:, 0:size] + both[:, size : 2 * size] + short_dot(low, factor_high, (1, 1))).T
        if n == 0:
            left = jnp.where(lane < 192, left[0:32], left[32:64])
        part[4 * n : 4 * n + 4] = left.reshape(4, 8, 384)
        if n == 0:
            pl.semaphore_wait(barrier, 18)

        @pl.loop(1, 16)
        def _(d):
            @pl.when((shard_peer(d) >= 4 * n) & (shard_peer(d) < 4 * n + 4))
            def _():
                part_copy(d).start()

        if n == 0:
            for half in range(2):
                for d in range(1, 4):
                    first_copy(half, d).start()

    def power_copy(d):
        return remote(
            power.at[me], power.at[me], power_send.at[d], power_recv.at[d],
            {"shard": shard_peer(d)},
        )

    @pl.when(me < CHUNKS)
    def _():
        @pl.loop(1, 16)
        def _(d):
            part_copy(d).wait_recv()

        total = part[me]
        for d in range(1, 16):
            total += part_slots[d]
        power[me] = total

        @pl.loop(1, 16)
        def _(d):
            power_copy(d).start()

    @pl.loop(1, 16)
    def _(d):
        @pl.when(shard_source(d) < CHUNKS)
        def _():
            remote(
                power.at[0], power.at[0], power_send.at[d], power_recv.at[d],
                {"shard": shard_peer(d)},
            ).wait_recv()

    zeros = jnp.zeros((RANK, 384), jnp.float32)
    spread = []
    for n in range(3):
        left = power[4 * n : 4 * n + 4].reshape(RANK, 384)
        if n == 0:
            spread.append(
                jnp.concatenate(
                    [jnp.where(lane < 192, left, 0.0), jnp.where(lane < 192, 0.0, left), zeros], axis=0
                )
            )
        else:
            spread.append(jnp.concatenate([zeros, zeros, left], axis=0))
    blocks, _ = block_mask(96)
    gram = dot(spread[0], spread[0], (1, 1))
    gram += dot(spread[1], spread[1], (1, 1))
    gram += dot(spread[2], spread[2], (1, 1))
    gram_slots[my_tensor] = gram[0:32] + gram[32:64] + gram[64:96]

    def gram_copy(d):
        return remote(
            gram_slots.at[my_tensor], gram_slots.at[my_tensor], gram_send.at[d], gram_recv.at[d],
            {"tensor": lax.rem(my_tensor + d, 4)},
        )

    for d in range(1, 4):
        gram_copy(d).start()

    own_base.wait()
    for half in range(2):
        for d in range(1, 4):
            first_copy(half, d).wait_recv()
    for half in range(2):
        for d in range(1, 4):
            second_copy(half, d).start()

    @pl.loop(1, 16)
    def _(d):
        small_copy(d).start()

    for d in range(1, 4):
        gram_copy(d).wait_recv()
    total = (gram_slots[0] + gram_slots[1]) + (gram_slots[2] + gram_slots[3])
    root = inverse_root(jnp.where(blocks, jnp.concatenate([total, total, total], axis=0), 0.0))

    terms = []
    for n in range(3):
        at = slice(n * 384, n * 384 + 384)
        used = slice(0, 64) if n == 0 else slice(64, 96)
        ortho = dot(root, spread[n], (0, 0))
        ortho_out[:, at] = ortho
        ortho_high, ortho_low = halves(ortho[used])
        size = 64 if n == 0 else 32
        both = short_dot(jnp.concatenate([ortho_high, ortho_low], axis=0), merged_high[at], (1, 0))
        terms.append(
            both[0:size] + both[size : 2 * size] + short_dot(ortho_high, merged_low[at], (1, 0))
        )
    back_part[0:8] = terms[0].reshape(8, 8, 768)
    back_part[8:12] = (terms[1] + terms[2]).reshape(4, 8, 768)

    def bpart_copy(d):
        return remote(
            back_part.at[lax.rem(shard_peer(d), CHUNKS)], back_slots.at[d], bpart_send.at[d],
            bpart_recv.at[d], {"shard": shard_peer(d)},
        )

    def piece_copy(d):
        return remote(
            back_pieces.at[my_tensor], back_pieces.at[my_tensor], piece_send.at[d],
            piece_recv.at[d], {"tensor": lax.rem(my_tensor + d, 4)},
        )

    def back_copy(d):
        return remote(
            back.at[me], back.at[me], back_send.at[d], back_recv.at[d],
            {"shard": shard_peer(d)},
        )

    @pl.loop(1, 16)
    def _(d):
        @pl.when(shard_peer(d) < CHUNKS)
        def _():
            bpart_copy(d).start()

    @pl.when(me < CHUNKS)
    def _():
        @pl.loop(1, 16)
        def _(d):
            bpart_copy(d).wait_recv()

        total = back_part[me]
        for d in range(1, 16):
            total += back_slots[d]
        back_pieces[my_tensor] = total
        for d in range(1, 4):
            piece_copy(d).start()
        for d in range(1, 4):
            piece_copy(d).wait_recv()
        total = (back_pieces[0] + back_pieces[1]) + (back_pieces[2] + back_pieces[3])
        back[me] = total * (1.0 / 16.0)

        @pl.loop(1, 16)
        def _(d):
            back_copy(d).start()

    @pl.loop(1, 16)
    def _(d):
        @pl.when(shard_source(d) < CHUNKS)
        def _():
            remote(
                back.at[0], back.at[0], back_send.at[d], back_recv.at[d],
                {"shard": shard_peer(d)},
            ).wait_recv()

    total = back[...].reshape(96, 768)
    back_out[...] = total
    root = inverse_root(jnp.where(blocks, dot(total, total, (1, 1)), 0.0))
    factor_out[...] = dot(root, total, (0, 0))

    @pl.loop(1, 16)
    def _(d):
        small_copy(d).wait_recv()

    total = small_slots[0]
    for n in range(1, 16):
        total += small_slots[n]
    small_out[...] = total

    for half in range(2):
        for d in range(1, 4):
            second_copy(half, d).wait_recv()

    @pl.loop(1, 16)
    def _(d):
        small_copy(d).wait_send()

        @pl.when(shard_peer(d) < CHUNKS)
        def _():
            part_copy(d).wait_send()
            bpart_copy(d).wait_send()

    @pl.when(me < CHUNKS)
    def _():
        @pl.loop(1, 16)
        def _(d):
            power_copy(d).wait_send()
            back_copy(d).wait_send()

        for d in range(1, 4):
            piece_copy(d).wait_send()

    for d in range(1, 4):
        gram_copy(d).wait_send()
        for half in range(2):
            first_copy(half, d).wait_send()
            second_copy(half, d).wait_send()


def exchange(*operands):
    any_spec = pl.BlockSpec(memory_space=pl.ANY)
    vmem_spec = pl.BlockSpec(memory_space=pltpu.VMEM)
    dma = pltpu.SemaphoreType.DMA
    f32 = jnp.float32
    return pl.pallas_call(
        exchange_kernel,
        out_shape=(
            jax.ShapeDtypeStruct((96, 1152), f32),
            jax.ShapeDtypeStruct((96, 768), f32),
            jax.ShapeDtypeStruct((96, 768), f32),
            jax.ShapeDtypeStruct((8, 256), f32),
            jax.ShapeDtypeStruct((4, 4, 2, 24, 1152), f32),
        ),
        in_specs=[any_spec] * 10 + [vmem_spec] * 2,
        out_specs=(vmem_spec, vmem_spec, vmem_spec, vmem_spec, any_spec),
        scratch_shapes=[
            pltpu.VMEM((1152, 768), f32),
            pltpu.VMEM((1152, 768), f32),
            pltpu.VMEM((1152, 768), jnp.bfloat16),
            pltpu.VMEM((1152, 768), jnp.bfloat16),
            pltpu.VMEM((96, 768), f32),
            pltpu.VMEM((2, 48, 192), f32),
            pltpu.VMEM((48, 768), f32),
            pltpu.VMEM((2, 48, 192), f32),
            pltpu.VMEM((48, 768), f32),
            pltpu.VMEM((2, 24, 1152), f32),
            pltpu.VMEM((12, 8, 384), f32),
            pltpu.VMEM((16, 8, 384), f32),
            pltpu.VMEM((12, 8, 384), f32),
            pltpu.VMEM((4, 32, 96), f32),
            pltpu.VMEM((12, 8, 768), f32),
            pltpu.VMEM((16, 8, 768), f32),
            pltpu.VMEM((4, 8, 768), f32),
            pltpu.VMEM((12, 8, 768), f32),
            pltpu.VMEM((16, 8, 256), f32),
            dma((3, 2)),
            dma((6,)),
            dma,
        ]
        + [dma((16,))] * 4
        + [dma((4,))] * 2
        + [dma((16,))] * 2
        + [dma((4,))] * 2
        + [dma((16,))] * 4
        + [dma((2, 4))] * 4,
        compiler_params=pltpu.CompilerParams(collective_id=0, has_side_effects=True),
        name="exchange",
    )(*operands)


ROWS = 128


def update_kernel(
    att_grads, att_errors, ff_grads, ff_errors, ortho, back, base,
    att_momentum, ff_momentum, att_master, ff_master, small, factor,
    gain_momentum, gain_weight, bias_momentum, bias_weight,
    att_errors_out, ff_errors_out, att_fresh_out, ff_fresh_out,
    att_momentum_out, ff_momentum_out, att_master_out, ff_master_out,
    gain_momentum_out, gain_weight_out, bias_momentum_out, bias_weight_out,
    att_factor_out, ff_factor_out,
):
    n = pl.program_id(0)
    at = pl.ds(pl.multiple_of(n * ROWS, ROWS), ROWS)

    def product(used):
        left_high, left_low = halves(ortho[used, at])
        right_high, right_low = halves(back[used])
        return short_dot(
            jnp.concatenate([left_high, left_high, left_low], axis=0),
            jnp.concatenate([right_high, right_low, right_high], axis=0),
            (0, 0),
        )

    @pl.when(n < 3)
    def _():
        approx = product(slice(0, 64))
        fresh = (base[...].T - learn_rate * approx).astype(jnp.bfloat16)
        att_errors_out[...] = att_grads[...] + att_errors[...] - approx
        att_fresh_out[...] = fresh

    @pl.when(n >= 3)
    def _():
        approx = product(slice(64, 96))
        fresh = (base[...].T - learn_rate * approx).astype(jnp.bfloat16)
        ff_errors_out[...] = ff_grads[...] + ff_errors[...] - approx
        ff_fresh_out[...] = fresh

    @pl.when(n == 0)
    def _():
        shard = lax.axis_index("shard")
        own_back = pltpu.roll(back[...], lax.rem(768 - 48 * shard, 768), 1)[:, 0:128]
        left_high, left_low = halves(own_back)
        right_high, right_low = halves(ortho[...])
        own = short_dot(
            jnp.concatenate([left_high, left_high, left_low], axis=0),
            jnp.concatenate([right_high, right_low, right_high], axis=0),
            (0, 0),
        )[0:48]
        step = learn_rate * decay_rate
        att_own = own[:, 0:384]
        for m in range(2):
            piece = (att_own if m == 0 else pltpu.roll(att_own, 192, 1))[:, 0:192]
            att_momentum_out[m] = decay_rate * att_momentum[m] + piece
            att_master_out[m] = att_master[m] - step * att_momentum[m] - learn_rate * piece
        piece = own[:, 384:1152]
        ff_momentum_out[...] = decay_rate * ff_momentum[...] + piece
        ff_master_out[...] = ff_master[...] - step * ff_momentum[...] - learn_rate * piece
        gain = decay_rate * gain_momentum[...] + small[0:1, 0:192] * (1.0 / 16.0)
        gain_momentum_out[...] = gain
        gain_weight_out[...] = gain_weight[...] - learn_rate * gain
        bias = decay_rate * bias_momentum[...] + small[1:4, 0:32] * (1.0 / 16.0)
        bias_momentum_out[...] = bias
        bias_weight_out[...] = bias_weight[...] - learn_rate * bias
        att_factor_out[...] = factor[0:64]
        ff_factor_out[...] = factor[64:96]


def update(*operands):
    def att_block(n):
        return jnp.minimum(n, 2), 0

    def ff_block(n):
        return jnp.maximum(n - 3, 0), 0

    def whole(*shape):
        return pl.BlockSpec(shape, lambda n: (0,) * len(shape))

    att = pl.BlockSpec((ROWS, 768), att_block)
    ff = pl.BlockSpec((ROWS, 768), ff_block)
    states = [whole(2, 48, 192), whole(48, 768)]
    vectors = [whole(1, 192)] * 2 + [whole(3, 32)] * 2
    shapes = [
        ((384, 768), jnp.float32), ((768, 768), jnp.float32),
        ((384, 768), jnp.bfloat16), ((768, 768), jnp.bfloat16),
        ((2, 48, 192), jnp.float32), ((48, 768), jnp.float32),
        ((2, 48, 192), jnp.float32), ((48, 768), jnp.float32),
        ((1, 192), jnp.float32), ((1, 192), jnp.float32),
        ((3, 32), jnp.float32), ((3, 32), jnp.float32),
        ((64, 768), jnp.float32), ((32, 768), jnp.float32),
    ]
    return pl.pallas_call(
        update_kernel,
        grid=(1152 // ROWS,),
        out_shape=[jax.ShapeDtypeStruct(*shape) for shape in shapes],
        in_specs=[att, att, ff, ff, whole(96, 1152), whole(96, 768)]
        + [pl.BlockSpec((768, ROWS), lambda n: (0, n))]
        + states + states + [whole(8, 256), whole(96, 768)] + vectors,
        out_specs=[att, ff, att, ff] + states + states + vectors
        + [whole(64, 768), whole(32, 768)],
        name="update",
    )(*operands)


def per_device(
    attention_grads,
    feedforward_grads,
    attention_errors,
    feedforward_errors,
    attention_factor,
    feedforward_factor,
    attention_momentum,
    feedforward_momentum,
    attention_master,
    feedforward_master,
    gain_grads,
    bias_grads,
    gain_momentum,
    gain_weight,
    bias_momentum,
    bias_weight,
):
    att_grads = attention_grads.reshape(384, 768)
    ff_grads = feedforward_grads.reshape(768, 768)
    att_errors = attention_errors.reshape(384, 768)
    ff_errors = feedforward_errors.reshape(768, 768)
    states = (
        jnp.swapaxes(attention_momentum, 1, 2), feedforward_momentum[0].T,
        jnp.swapaxes(attention_master, 1, 2), feedforward_master[0].T,
    )
    ortho, back, factor_new, small_total, base_full = exchange(
        att_grads, ff_grads, att_errors, ff_errors,
        jnp.swapaxes(attention_factor, 1, 2).reshape(64, 768), feedforward_factor[0].T,
        *states, gain_grads.reshape(1, 192), jnp.swapaxes(bias_grads, 0, 1),
    )
    (
        att_errors_new, ff_errors_new, att_fresh, ff_fresh,
        att_momentum_new, ff_momentum_new, att_master_new, ff_master_new, *vectors,
        att_factor_new, ff_factor_new,
    ) = update(
        att_grads, att_errors, ff_grads, ff_errors, ortho, back, base_full.reshape(768, 1152),
        *states, small_total, factor_new, gain_momentum, gain_weight, bias_momentum, bias_weight,
    )
    return (
        att_errors_new.reshape(1, 2, 192, 768),
        ff_errors_new.reshape(1, 1, 768, 768),
        jnp.swapaxes(att_factor_new.reshape(2, 32, 768), 1, 2),
        ff_factor_new.T[None],
        jnp.swapaxes(att_momentum_new, 1, 2),
        ff_momentum_new.T[None],
        jnp.swapaxes(att_master_new, 1, 2),
        ff_master_new.T[None],
        att_fresh.reshape(2, 192, 768),
        ff_fresh.reshape(1, 768, 768),
        *vectors,
    )


def solution(mesh):
    placed = (
        P("shard", "section", "tensor", None),
        P("shard", "section", "tensor", None),
        P("shard", "section", "tensor", None),
        P("shard", "section", "tensor", None),
        P("section", None, None),
        P("section", None, None),
        P("section", "tensor", "shard"),
        P("section", "tensor", "shard"),
        P("section", "tensor", "shard"),
        P("section", "tensor", "shard"),
        P("shard", "section", "tensor"),
        P("shard", "tensor", None),
        P("section", "tensor"),
        P("section", "tensor"),
        P("tensor", None),
        P("tensor", None),
    )
    return jax.shard_map(
        per_device,
        mesh=mesh,
        in_specs=placed,
        out_specs=(
            P("shard", "section", "tensor", None),
            P("shard", "section", "tensor", None),
            P("section", None, None),
            P("section", None, None),
            P("section", "tensor", "shard"),
            P("section", "tensor", "shard"),
            P("section", "tensor", "shard"),
            P("section", "tensor", "shard"),
            P("section", "tensor", None),
            P("section", "tensor", None),
            P("section", "tensor"),
            P("section", "tensor"),
            P("tensor", None),
            P("tensor", None),
        ),
        check_vma=False,
    )
```
